256 devices in a mesh: band: 64 (over z, y_hi, x), mem: 4 (over y_lo, core).
Axes of the slice: x: 4, y: 4 (y_hi: 2, y_lo: 2; y = y_hi * 2 + y_lo), z: 8, core: 2. Of those that a mesh axis runs over, the one named last changes fastest.
Arguments:
- coef: float32 [2, 512, 128, 2, 512], P(None, 'band', 'mem'), may hold values from -6 to 6
- perturb: bfloat16 [768, 128, 2, 1536], P('band', 'mem'), may hold values from -6 to 6
- weight: float32 [768, 2, 1536], P('band'), may hold values from 1 to 10
- table: bfloat16 [512, 512, 768], P('band'), may hold values from -0.0078125 to 0.0078125
- wave_map: int32 [512], replicated, may hold values from 0 to 511, each once
- lat_map: int32 [768], replicated, may hold values from 0 to 767, each once
Outputs:
- increment: float32 [768, 2, 1536], P('band')
- product: float32 [2, 512, 128, 2, 512], P(None, 'band', 'mem')
The draws below stay inside these ranges and needn't reach their ends.
Inputs may be any that keep to these rules, and one draw needn't show every extreme that they name: A permutation: spectral row r holds zonal wavenumber wave_map[r]. A permutation: grid row s holds Gaussian latitude lat_map[s]; the last dimension of table stands in natural latitude order.
All inputs are finite; a program needn't handle non-finite values.
Results may differ from the reference program's by a relative error of at most 0.0048.
Values may be sent and summed in bfloat16 or wider, within the bound.
A program may use at most 128 MiB of HBM per device.

```python
import math
import jax
import jax.numpy as jnp
from jax import lax

M = 512
LAT = 768
LON = 1536
LEV = 2
MEMBERS = 128


def block_scale(stream_key, extent, split, smallest, largest):
    def one(position, blocks):
        draws = jax.random.uniform(jax.random.fold_in(jax.random.fold_in(stream_key, 6), position), (blocks,), jnp.float32, smallest / len(split), largest / len(split))
        return jnp.repeat(jnp.exp(draws), extent[position] // blocks).reshape((-1,) + (1,) * (len(extent) - position - 1))

    gain = one(*split[0])
    for cut in split[1:]:
        gain = gain * one(*cut)
    return gain


def noise(rng, shape, deviation, bound, pieces=(), held_as=jnp.bfloat16):
    result = jax.random.normal(rng, shape, jnp.float32) * deviation
    if len(pieces) > 0:
        result = block_scale(rng, shape, pieces, -0.22, 0.18) * result
    return jnp.clip(result, min=-bound, max=bound).astype(held_as)


def setup_inputs(seed: int = 0) -> dict:
    seeds = jax.random.split(jax.random.key(seed), 7)
    return {
        "coef": noise(seeds[0], (2, M, MEMBERS, LEV, M), 1.0, 6.0, ((1, 64), (2, 4)), jnp.float32),
        "perturb": noise(seeds[1], (LAT, MEMBERS, LEV, LON), 1.0, 6.0, ((0, 64), (1, 4))),
        "weight": jnp.clip(jnp.exp(math.log(10.0) - 2.3025851 * jax.random.uniform(seeds[2], (LAT, LEV, LON), jnp.float32) ** block_scale(seeds[2], (LAT, LEV, LON), ((0, 64),), -0.2, 0.2)), 1.0, 10.0),
        "table": noise(seeds[3], (M, M, LAT), (2 * M * M) ** -0.5, 0.0078125, ((0, 64),)),
        "wave_map": jax.random.permutation(seeds[4], M).astype(jnp.int32),
        "lat_map": jax.random.permutation(seeds[5], LAT).astype(jnp.int32),
    }


def make_tables(table, wave_map, lat_map, lon):
    nwave = table.shape[1]
    start_offsets = jnp.arange(nwave, dtype=jnp.int32)
    valid = (start_offsets[None, :] < (nwave - wave_map)[:, None]).astype(jnp.float32)
    loc_table = (jnp.take(table, lat_map, axis=2).astype(jnp.float32) * valid[:, :, None]).astype(jnp.bfloat16)
    columns = jnp.arange(lon, dtype=jnp.int32)
    phase = wave_map[:, None] * columns[None, :] % lon
    angle = phase.astype(jnp.float32) * (2.0 * math.pi / lon)
    scale_multiplier = jnp.where(wave_map == 0, 1.0, 2.0).astype(jnp.float32)[:, None]
    fourier_table = jnp.stack([scale_multiplier * jnp.cos(angle), -scale_multiplier * jnp.sin(angle)], axis=0).astype(jnp.bfloat16)
    return (valid, loc_table, fourier_table)

def reference(coef, perturb, weight, table, wave_map, lat_map):
    ensemble_members = coef.shape[2]
    lon = perturb.shape[-1]
    valid, loc_table, fourier_table = make_tables(table, wave_map, lat_map, lon)
    scale = 1.0 / math.sqrt(ensemble_members - 1)
    masked = coef * valid[None, :, None, None, :]
    spec = masked.astype(jnp.bfloat16)
    fields = jnp.einsum('crklj,rjs->crskl', spec.astype(jnp.float32), loc_table.astype(jnp.float32)).astype(jnp.bfloat16)
    grid = jnp.einsum('crskl,crx->sklx', fields.astype(jnp.float32), fourier_table.astype(jnp.float32))
    increment = lax.optimization_barrier(jnp.sum(perturb.astype(jnp.float32) * grid, axis=1)) * scale
    gradient = weight * increment
    adjoint_grid = (perturb.astype(jnp.float32) * gradient[:, None] * scale).astype(jnp.bfloat16)
    adjoint_fields = jnp.einsum('sklx,crx->crskl', adjoint_grid.astype(jnp.float32), fourier_table.astype(jnp.float32)).astype(jnp.bfloat16)
    back = jnp.einsum('crskl,rjs->crklj', adjoint_fields.astype(jnp.float32), loc_table.astype(jnp.float32))
    product = masked + back
    return (increment, product)
```

```python
import functools
import math

import jax
import jax.numpy as jnp
from jax import lax
from jax.experimental import pallas as pl
from jax.experimental.pallas import tpu as pltpu
from jax.sharding import PartitionSpec as P

MESH = pl.DeviceIdType.MESH
F32 = jnp.float32
BF16 = jnp.bfloat16

NCH = 3


def body_a(
    wave_ref, lat_ref, coef_hbm, pert_hbm, w_hbm, table_hbm,
    inc_out, back_out,
    tab_v, coef_v, pert_v, w_v, spec32, nat, send_f, recv_f, xt, dft, pert32, w8, part, recv_i, inc_v, adj, send_b,
    in_sem, tab_sem, fs_sem, fr_sem, is_sem, ir_sem, bs_sem, br_sem, loc_sem, out_sem,
):
    band = lax.axis_index("band")
    mem = lax.axis_index("mem")
    nb, nm = 64, 4
    nwave, nlat, lon = 512, 768, 1536

    tcopies = [
        pltpu.make_async_copy(table_hbm.at[r], tab_v.at[r], tab_sem.at[r]) for r in range(8)
    ]
    c_copy = pltpu.make_async_copy(coef_hbm, coef_v, in_sem.at[0])
    p_copy = pltpu.make_async_copy(pert_hbm, pert_v, in_sem.at[1])
    w_copy = pltpu.make_async_copy(w_hbm, w_v, in_sem.at[2])
    c_copy.start()
    for t in tcopies:
        t.start()
    p_copy.start()
    w_copy.start()

    barrier = pltpu.get_barrier_semaphore()

    def greet(i, c):
        pl.semaphore_signal(
            barrier, inc=1, device_id=(lax.rem(band + i, nb), mem), device_id_type=MESH
        )
        return c

    lax.fori_loop(1, nb, greet, 0)
    for i in range(1, nm):
        pl.semaphore_signal(
            barrier, inc=1, device_id=(band, lax.rem(mem + i, nm)), device_id_type=MESH
        )

    z, y, x = band // 8, lax.rem(band // 4, 2), lax.rem(band, 4)

    def peer(i):
        a, b = lax.rem(i, 8), 7 - i // 8
        dz = jnp.where(lax.rem(a, 2) == 0, 4 - a // 2, 5 + a // 2)
        dz = jnp.where(a == 7, 0, dz)
        dy, dx = b // 4, lax.rem(b, 4)
        return (lax.rem(z + dz, 8) * 2 + lax.rem(y + dy, 2)) * 4 + lax.rem(x + dx, 4)

    c_copy.wait()
    lane_j = lax.broadcasted_iota(jnp.int32, (2, nwave), 1)

    def to_spec(r, c):
        limit = nwave - wave_ref[band * 8 + r]
        keep = lane_j < limit
        for part_i in range(2):
            for k in range(32):
                v = coef_v[part_i, r, k]
                spec32[r, pl.ds(part_i * 64 + 2 * k, 2), :] = jnp.where(keep, v, 0.0)
        return c

    lax.fori_loop(0, 8, to_spec, 0)

    for r in range(8):
        tcopies[r].wait()
        f = jnp.dot(spec32[r].astype(BF16), tab_v[r], preferred_element_type=F32)
        nat.reshape(nlat * 8, 128)[pl.ds(r, nlat, stride=8), :] = f.T

    pl.semaphore_wait(barrier, nb - 1 + nm - 1)

    lane = lax.broadcasted_iota(jnp.int32, (8, 128), 1)
    left = lane < 64

    def send_chunk(buf, ch, dst, s_sem, r_sem):
        def one(i, c):
            e = peer(i)
            pltpu.make_async_remote_copy(
                buf.at[ch, e], dst.at[ch, band], s_sem.at[ch], r_sem.at[ch],
                device_id=(e, mem), device_id_type=MESH,
            ).start()
            return c

        lax.fori_loop(0, nb - 1, one, 0)

    def rest(buf, ch, dst, s_sem, r_sem):
        return pltpu.make_async_remote_copy(
            buf.at[ch, pl.ds(0, nb - 1)], dst.at[ch, pl.ds(0, nb - 1)], s_sem.at[ch], r_sem.at[ch],
            device_id=(lax.rem(band + 1, nb), mem), device_id_type=MESH,
        )

    def row(s):
        return nat[lat_ref[s]]

    for ch in range(NCH):

        def build(e, c):
            for p in range(2):
                s0 = e * 12 + ch * 4 + 2 * p
                a, b = row(s0), row(s0 + 1)
                lo = jnp.where(left, a, pltpu.roll(b, 64, 1))
                hi = jnp.where(left, pltpu.roll(a, 64, 1), b)
                send_f[ch, e, :, p * 128 : (p + 1) * 128] = jnp.concatenate(
                    [lo, hi], axis=0
                ).astype(BF16)
            return c

        lax.fori_loop(0, nb, build, 0)
        pltpu.make_async_copy(send_f.at[ch, band], recv_f.at[ch, band], loc_sem.at[ch]).start()
        send_chunk(send_f, ch, recv_f, fs_sem, fr_sem)

    row8 = lax.broadcasted_iota(jnp.int32, (8, 128), 0)

    def fourier(d, c):
        m = jnp.zeros((8, 128), jnp.int32)
        for i in range(8):
            m = jnp.where(row8 == i, wave_ref[d * 8 + i], m)
        low = lax.rem(m * lane, lon).astype(F32) * (2.0 * math.pi / lon)
        high = (lax.rem(m * lane, 12) * 128).astype(F32) * (2.0 * math.pi / lon)
        cb, sb = jnp.cos(low), jnp.sin(low)
        f = jnp.where(m == 0, 1.0, 2.0)
        fc, fs = f * jnp.cos(high), f * jnp.sin(high)
        for xb in range(12):
            ca = jnp.broadcast_to(fc[:, xb : xb + 1], (8, 128))
            sa = jnp.broadcast_to(fs[:, xb : xb + 1], (8, 128))
            dft[pl.ds(pl.multiple_of(d * 16, 16), 16), xb * 128 : (xb + 1) * 128] = (
                jnp.concatenate([ca * cb - sa * sb, -(sa * cb + ca * sb)], axis=0).astype(BF16)
            )
        return c

    lax.fori_loop(0, nb, fourier, 0)

    p_copy.wait()
    w_copy.wait()

    def to_rows(s, c):
        for k in range(32):
            pert32[s, pl.ds(2 * k, 2), :] = pert_v[s, k].astype(F32)
        return c

    lax.fori_loop(0, 12, to_rows, 0)
    for s in range(12):
        w8[s // 4, pl.ds(2 * (s % 4), 2), :] = w_v[s]

    scale = 1.0 / math.sqrt(32 * nm - 1)
    xw = 512

    for ch in range(NCH):
        pltpu.make_async_copy(send_f.at[ch, band], recv_f.at[ch, band], loc_sem.at[ch]).wait()
        rest(send_f, ch, recv_f, fs_sem, fr_sem).wait_recv()
        xt[...] = recv_f[ch].reshape(1024, 256).T

        def forward(i, c):
            cols = pl.ds(pl.multiple_of(i * xw, xw), xw)
            g = jnp.dot(xt[...], dft[:, cols], preferred_element_type=F32)
            for s in range(4):
                t = pert32[ch * 4 + s, :, cols] * g[s * 64 : (s + 1) * 64]
                t = jnp.sum(t.reshape(8, 8, xw), axis=0)
                t = t + pltpu.roll(t, 4, 0)
                t = t + pltpu.roll(t, 6, 0)
                part[ch, pl.ds(2 * s, 2), cols] = t[0:2]
            return c

        lax.fori_loop(0, lon // xw, forward, 0)

        copies = [
            pltpu.make_async_remote_copy(
                part.at[ch], recv_i.at[ch, i - 1], is_sem.at[ch, i - 1], ir_sem.at[ch, i - 1],
                device_id=(band, lax.rem(mem + i, nm)), device_id_type=MESH,
            )
            for i in range(1, nm)
        ]
        for cp in copies:
            cp.start()
        for cp in copies:
            cp.wait_recv()
        g0, g1, g2, g3 = part[ch], recv_i[ch, 0], recv_i[ch, 1], recv_i[ch, 2]
        inc = ((g0 + g2) + (g1 + g3)) * scale
        inc_v[pl.ds(8 * ch, 8), :] = inc
        w8[ch] = w8[ch] * inc * scale

        def backward(s):
            g = w8[ch, 2 * s : 2 * s + 2, :]
            g = jnp.concatenate([g] * 4, axis=0)
            a = pert32[ch * 4 + s].reshape(8, 8, lon) * g[None]
            adj[s * 64 : (s + 1) * 64, :] = a.reshape(64, lon).astype(BF16)

        for s in range(4):
            backward(s)

        def back(i, c):
            rows = pl.ds(pl.multiple_of(i * 256, 256), 256)
            v = lax.dot_general(
                dft[rows, :], adj[...], (((1,), (1,)), ((), ())), preferred_element_type=F32
            )
            send_b[ch, pl.ds(pl.multiple_of(i * 16, 16), 16)] = v.astype(BF16).reshape(16, 16, 256)
            return c

        lax.fori_loop(0, 4, back, 0)
        pltpu.make_async_copy(
            send_b.at[ch, band], back_out.at[ch, band], loc_sem.at[NCH + ch]
        ).start()
        send_chunk(send_b, ch, back_out, bs_sem, br_sem)

    for s in range(12):
        inc_out[s] = inc_v[pl.ds(2 * s, 2), :]

    for ch in range(NCH):
        rest(send_f, ch, recv_f, fs_sem, fr_sem).wait_send()
        for i in range(1, nm):
            pltpu.make_async_remote_copy(
                part.at[ch], recv_i.at[ch, i - 1], is_sem.at[ch, i - 1], ir_sem.at[ch, i - 1],
                device_id=(band, lax.rem(mem + i, nm)), device_id_type=MESH,
            ).wait_send()
        pltpu.make_async_copy(
            send_b.at[ch, band], back_out.at[ch, band], loc_sem.at[NCH + ch]
        ).wait()
        rest(send_b, ch, back_out, bs_sem, br_sem).wait()


def body_b(wave_ref, lat_ref, back_ref, table_ref, coef_ref, out_ref, nat, acc):
    r = pl.program_id(0)
    nlat, nwave = 768, 512
    lane = lax.broadcasted_iota(jnp.int32, (8, 128), 1)
    left = lane < 64

    @pl.when(r == 0)
    def _():
        def put(s, v):
            nat[pl.ds(pl.multiple_of(lat_ref[s] * 8, 8), 8), :] = v

        for ch in range(NCH):

            def open_up(e, c):
                for p in range(2):
                    s0 = e * 12 + ch * 4 + 2 * p
                    t = back_ref[ch, e, :, p * 128 : (p + 1) * 128].astype(F32)
                    lo, hi = t[0:8], t[8:16]
                    put(s0, jnp.where(left, lo, pltpu.roll(hi, 64, 1)))
                    put(s0 + 1, jnp.where(left, pltpu.roll(lo, 64, 1), hi))
                return c

            lax.fori_loop(0, 64, open_up, 0)

    a = nat[pl.ds(r, nlat, stride=8), :].astype(BF16)
    back = lax.dot_general(
        a, table_ref[0], (((0,), (1,)), ((), ())), preferred_element_type=F32
    )
    acc[...] = back
    keep = lax.broadcasted_iota(jnp.int32, (2, nwave), 1) < nwave - wave_ref[r]
    for c in range(2):
        for k in range(32):
            out_ref[c, 0, k] = jnp.where(
                keep, coef_ref[c, 0, k] + acc[pl.ds(c * 64 + 2 * k, 2), :], 0.0
            )


def body(coef, perturb, weight, table, wave_map, lat_map):
    any_ = pl.BlockSpec(memory_space=pl.ANY)
    smem = pl.BlockSpec(memory_space=pltpu.SMEM)
    dma = pltpu.SemaphoreType.DMA
    inc, back = pl.pallas_call(
        body_a,
        out_shape=(
            jax.ShapeDtypeStruct((12, 2, 1536), F32),
            jax.ShapeDtypeStruct((NCH, 64, 16, 256), BF16),
        ),
        in_specs=[smem, smem, any_, any_, any_, any_],
        out_specs=(pl.BlockSpec(memory_space=pltpu.VMEM), any_),
        scratch_shapes=[
            pltpu.VMEM((8, 512, 768), BF16),
            pltpu.VMEM((2, 8, 32, 2, 512), F32),
            pltpu.VMEM((12, 32, 2, 1536), BF16),
            pltpu.VMEM((12, 2, 1536), F32),
            pltpu.VMEM((8, 128, 512), F32),
            pltpu.VMEM((768, 8, 128), F32),
            pltpu.VMEM((NCH, 64, 16, 256), BF16),
            pltpu.VMEM((NCH, 64, 16, 256), BF16),
            pltpu.VMEM((256, 1024), BF16),
            pltpu.VMEM((1024, 1536), BF16),
            pltpu.VMEM((12, 64, 1536), F32),
            pltpu.VMEM((NCH, 8, 1536), F32),
            pltpu.VMEM((NCH, 8, 1536), F32),
            pltpu.VMEM((NCH, 3, 8, 1536), F32),
            pltpu.VMEM((24, 1536), F32),
            pltpu.VMEM((256, 1536), BF16),
            pltpu.VMEM((NCH, 64, 16, 256), BF16),
            dma((3,)),
            dma((8,)),
            dma((NCH,)),
            dma((NCH,)),
            dma((NCH, 3)),
            dma((NCH, 3)),
            dma((NCH,)),
            dma((NCH,)),
            dma((2 * NCH,)),
            dma,
        ],
        compiler_params=pltpu.CompilerParams(
            collective_id=0, has_side_effects=True, vmem_limit_bytes=60 * 1024 * 1024
        ),
        name="transforms",
    )(wave_map, lat_map, coef, perturb, weight, table)
    own = lax.dynamic_slice_in_dim(wave_map, lax.axis_index("band") * 8, 8)
    product = pl.pallas_call(
        body_b,
        out_shape=jax.ShapeDtypeStruct((2, 8, 32, 2, 512), F32),
        grid=(8,),
        in_specs=[
            smem,
            smem,
            pl.BlockSpec((NCH, 64, 16, 256), lambda r: (0, 0, 0, 0)),
            pl.BlockSpec((1, 512, 768), lambda r: (r, 0, 0)),
            pl.BlockSpec((2, 1, 32, 2, 512), lambda r: (0, r, 0, 0, 0)),
        ],
        out_specs=pl.BlockSpec((2, 1, 32, 2, 512), lambda r: (0, r, 0, 0, 0)),
        scratch_shapes=[pltpu.VMEM((768 * 8, 128), F32), pltpu.VMEM((128, 512), F32)],
        compiler_params=pltpu.CompilerParams(vmem_limit_bytes=60 * 1024 * 1024),
        name="product",
    )(own, lat_map, back, table, coef)
    return inc, product


def solution(mesh):
    in_specs = (
        P(None, "band", "mem", None, None),
        P("band", "mem", None, None),
        P("band", None, None),
        P("band", None, None),
        P(),
        P(),
    )
    out_specs = (P("band", None, None), P(None, "band", "mem", None, None))
    return jax.shard_map(body, mesh=mesh, in_specs=in_specs, out_specs=out_specs, check_vma=False)
```

```python
import functools
import math

import jax
import jax.numpy as jnp
from jax import lax
from jax.experimental import pallas as pl
from jax.experimental.pallas import tpu as pltpu
from jax.sharding import PartitionSpec as P

MESH = pl.DeviceIdType.MESH
F32 = jnp.float32
BF16 = jnp.bfloat16

NCH = 3


def body_a(
    wave_ref, lat_ref, coef_hbm, pert_hbm, w_hbm, table_hbm,
    inc_out, prod_out,
    tab_v, coef_v, pert_v, w_v, spec32, nat, send_f, recv_f, xt, dft, pert32, w8, part, recv_i, inc_v, adj, send_b,
    recv_b, pick, opened, in_sem, tab_sem, fs_sem, fr_sem, is_sem, ir_sem, bs_sem, br_sem, loc_sem, out_sem,
):
    band = lax.axis_index("band")
    mem = lax.axis_index("mem")
    nb, nm = 64, 4
    nwave, nlat, lon = 512, 768, 1536

    tcopies = [
        pltpu.make_async_copy(table_hbm.at[r], tab_v.at[r], tab_sem.at[r]) for r in range(8)
    ]
    c_copy = pltpu.make_async_copy(coef_hbm, coef_v, in_sem.at[0])
    p_copy = pltpu.make_async_copy(pert_hbm, pert_v, in_sem.at[1])
    w_copy = pltpu.make_async_copy(w_hbm, w_v, in_sem.at[2])
    c_copy.start()
    for t in tcopies:
        t.start()
    p_copy.start()
    w_copy.start()

    barrier = pltpu.get_barrier_semaphore()

    def greet(i, c):
        pl.semaphore_signal(
            barrier, inc=1, device_id=(lax.rem(band + i, nb), mem), device_id_type=MESH
        )
        return c

    lax.fori_loop(1, nb, greet, 0)
    for i in range(1, nm):
        pl.semaphore_signal(
            barrier, inc=1, device_id=(band, lax.rem(mem + i, nm)), device_id_type=MESH
        )

    z, y, x = band // 8, lax.rem(band // 4, 2), lax.rem(band, 4)

    def peer(i):
        a, b = lax.rem(i, 8), 7 - i // 8
        dz = jnp.where(lax.rem(a, 2) == 0, 4 - a // 2, 5 + a // 2)
        dz = jnp.where(a == 7, 0, dz)
        dy, dx = b // 4, lax.rem(b, 4)
        return (lax.rem(z + dz, 8) * 2 + lax.rem(y + dy, 2)) * 4 + lax.rem(x + dx, 4)

    c_copy.wait()
    lane_j = lax.broadcasted_iota(jnp.int32, (2, nwave), 1)

    def to_spec(r, c):
        limit = nwave - wave_ref[band * 8 + r]
        keep = lane_j < limit
        for part_i in range(2):
            for k in range(32):
                v = coef_v[part_i, r, k]
                spec32[r, pl.ds(part_i * 64 + 2 * k, 2), :] = jnp.where(keep, v, 0.0)
        return c

    lax.fori_loop(0, 8, to_spec, 0)

    for r in range(8):
        tcopies[r].wait()
        f = jnp.dot(spec32[r].astype(BF16), tab_v[r], preferred_element_type=F32)
        nat.reshape(nlat * 8, 128)[pl.ds(r, nlat, stride=8), :] = f.T

    pl.semaphore_wait(barrier, nb - 1 + nm - 1)

    lane = lax.broadcasted_iota(jnp.int32, (8, 128), 1)
    left = lane < 64

    def send_chunk(buf, ch, dst, s_sem, r_sem):
        def one(i, c):
            e = peer(i)
            pltpu.make_async_remote_copy(
                buf.at[ch, e], dst.at[ch, band], s_sem.at[ch], r_sem.at[ch],
                device_id=(e, mem), device_id_type=MESH,
            ).start()
            return c

        lax.fori_loop(0, nb - 1, one, 0)

    def rest(buf, ch, dst, s_sem, r_sem):
        return pltpu.make_async_remote_copy(
            buf.at[ch, pl.ds(0, nb - 1)], dst.at[ch, pl.ds(0, nb - 1)], s_sem.at[ch], r_sem.at[ch],
            device_id=(lax.rem(band + 1, nb), mem), device_id_type=MESH,
        )

    def row(s):
        return nat[lat_ref[s]]

    for ch in range(NCH):

        def build(i):
            e = peer(i)
            for p in range(2):
                s0 = e * 12 + ch * 4 + 2 * p
                a, b = row(s0), row(s0 + 1)
                lo = jnp.where(left, a, pltpu.roll(b, 64, 1))
                hi = jnp.where(left, pltpu.roll(a, 64, 1), b)
                send_f[ch, e, :, p * 128 : (p + 1) * 128] = jnp.concatenate(
                    [lo, hi], axis=0
                ).astype(BF16)

        def send(i):
            e = peer(i)
            pltpu.make_async_remote_copy(
                send_f.at[ch, e], recv_f.at[ch, band], fs_sem.at[ch], fr_sem.at[ch],
                device_id=(e, mem), device_id_type=MESH,
            ).start()

        def step(g, c):
            for k in range(4):
                build(4 * g + k)
            for k in range(4):
                send(4 * g - 4 + k)
            return c

        for k in range(4):
            build(k)
        lax.fori_loop(1, nb // 4, step, 0)
        for k in range(3):
            send(nb - 4 + k)
        pltpu.make_async_copy(send_f.at[ch, band], recv_f.at[ch, band], loc_sem.at[ch]).start()

    row8 = lax.broadcasted_iota(jnp.int32, (8, 128), 0)

    def fourier(d, c):
        m = jnp.zeros((8, 128), jnp.int32)
        for i in range(8):
            m = jnp.where(row8 == i, wave_ref[d * 8 + i], m)
        low = lax.rem(m * lane, lon).astype(F32) * (2.0 * math.pi / lon)
        high = (lax.rem(m * lane, 12) * 128).astype(F32) * (2.0 * math.pi / lon)
        cb, sb = jnp.cos(low), jnp.sin(low)
        f = jnp.where(m == 0, 1.0, 2.0)
        fc, fs = f * jnp.cos(high), f * jnp.sin(high)
        for xb in range(12):
            ca = jnp.broadcast_to(fc[:, xb : xb + 1], (8, 128))
            sa = jnp.broadcast_to(fs[:, xb : xb + 1], (8, 128))
            dft[pl.ds(pl.multiple_of(d * 16, 16), 16), xb * 128 : (xb + 1) * 128] = (
                jnp.concatenate([ca * cb - sa * sb, -(sa * cb + ca * sb)], axis=0).astype(BF16)
            )
        return c

    lax.fori_loop(0, nb, fourier, 0, unroll=2)

    p_copy.wait()
    w_copy.wait()

    def to_rows(s, c):
        for k in range(32):
            pert32[s, pl.ds(2 * k, 2), :] = pert_v[s, k].astype(F32)
        return c

    lax.fori_loop(0, 12, to_rows, 0)
    for s in range(12):
        w8[s // 4, pl.ds(2 * (s % 4), 2), :] = w_v[s]

    scale = 1.0 / math.sqrt(32 * nm - 1)
    xw = 512

    for ch in range(NCH):
        pltpu.make_async_copy(send_f.at[ch, band], recv_f.at[ch, band], loc_sem.at[ch]).wait()
        rest(send_f, ch, recv_f, fs_sem, fr_sem).wait_recv()
        xt[...] = recv_f[ch].reshape(1024, 256).T

        def forward(i, c):
            cols = pl.ds(pl.multiple_of(i * xw, xw), xw)
            g = jnp.dot(xt[...], dft[:, cols], preferred_element_type=F32)
            for s in range(4):
                t = pert32[ch * 4 + s, :, cols] * g[s * 64 : (s + 1) * 64]
                t = jnp.sum(t.reshape(8, 8, xw), axis=0)
                t = t + pltpu.roll(t, 4, 0)
                t = t + pltpu.roll(t, 6, 0)
                part[ch, pl.ds(2 * s, 2), cols] = t[0:2]
            return c

        lax.fori_loop(0, lon // xw, forward, 0)

        copies = [
            pltpu.make_async_remote_copy(
                part.at[ch], recv_i.at[ch, i - 1], is_sem.at[ch, i - 1], ir_sem.at[ch, i - 1],
                device_id=(band, lax.rem(mem + i, nm)), device_id_type=MESH,
            )
            for i in range(1, nm)
        ]
        for cp in copies:
            cp.start()
        for cp in copies:
            cp.wait_recv()
        g0, g1, g2, g3 = part[ch], recv_i[ch, 0], recv_i[ch, 1], recv_i[ch, 2]
        inc = ((g0 + g2) + (g1 + g3)) * scale
        inc_v[pl.ds(8 * ch, 8), :] = inc
        w8[ch] = w8[ch] * inc * scale

        def backward(s):
            g = w8[ch, 2 * s : 2 * s + 2, :]
            g = jnp.concatenate([g] * 4, axis=0)
            a = pert32[ch * 4 + s].reshape(8, 8, lon) * g[None]
            adj[s * 64 : (s + 1) * 64, :] = a.reshape(64, lon).astype(BF16)

        for s in range(4):
            backward(s)

        def back(i, c):
            rows = pl.ds(pl.multiple_of(i * 256, 256), 256)
            v = lax.dot_general(
                dft[rows, :], adj[...], (((1,), (1,)), ((), ())), preferred_element_type=F32
            )
            send_b[ch, pl.ds(pl.multiple_of(i * 16, 16), 16)] = v.astype(BF16).reshape(16, 16, 256)
            return c

        lax.fori_loop(0, 4, back, 0)
        pltpu.make_async_copy(
            send_b.at[ch, band], recv_b.at[ch, band], loc_sem.at[NCH + ch]
        ).start()
        send_chunk(send_b, ch, recv_b, bs_sem, br_sem)

    for s in range(12):
        inc_out[s] = inc_v[pl.ds(2 * s, 2), :]

    def select(t, c):
        halves = []
        for h in range(2):
            m = jnp.zeros((8, 128), jnp.int32)
            for i in range(8):
                k = h * 8 + i
                m = jnp.where(row8 == i, lat_ref[(t % 16 * 4 + k // 4) * 12 + t // 16 * 4 + k % 4], m)
            halves.append(m)
        m = jnp.concatenate(halves, axis=0)
        lane16 = lax.broadcasted_iota(jnp.int32, (16, 128), 1)
        for b in range(nlat // 128):
            pick[pl.ds(pl.multiple_of(t * 16, 16), 16), b * 128 : (b + 1) * 128] = jnp.where(
                m == lane16 + b * 128, 1.0, 0.0
            ).astype(BF16)
        return c

    lax.fori_loop(0, nlat // 16, select, 0, unroll=2)

    def arrange(r, c):
        tab_v[r] = lax.dot_general(
            tab_v[r], pick[...], (((1,), (1,)), ((), ())), preferred_element_type=F32
        ).astype(BF16)
        return c

    lax.fori_loop(0, 8, arrange, 0)

    for ch in range(NCH):
        pltpu.make_async_copy(
            send_b.at[ch, band], recv_b.at[ch, band], loc_sem.at[NCH + ch]
        ).wait()
        rest(send_b, ch, recv_b, bs_sem, br_sem).wait_recv()

        def open_up(g, c):
            for k in range(8):
                e = g * 8 + k
                for p in range(2):
                    t = recv_b[ch, e, :, p * 128 : (p + 1) * 128].astype(F32)
                    lo, hi = t[0:8], t[8:16]
                    opened[e * 4 + 2 * p] = jnp.where(left, lo, pltpu.roll(hi, 64, 1))
                    opened[e * 4 + 2 * p + 1] = jnp.where(left, pltpu.roll(lo, 64, 1), hi)
            return c

        lax.fori_loop(0, nb // 8, open_up, 0)

        for r in range(8):
            a = opened.reshape(2048, 128)[pl.ds(r, 256, stride=8), :].astype(BF16)
            v = lax.dot_general(
                a, tab_v[r, :, ch * 256 : (ch + 1) * 256], (((0,), (1,)), ((), ())),
                preferred_element_type=F32,
            )
            if ch < NCH - 1:
                spec32[r] += v
            else:
                keep = lax.broadcasted_iota(jnp.int32, (128, nwave), 1) < nwave - wave_ref[band * 8 + r]
                spec32[r] = jnp.where(keep, spec32[r] + v, 0.0)
                pltpu.make_async_copy(spec32.at[r], prod_out.at[r], out_sem.at[r]).start()

    for ch in range(NCH):
        rest(send_f, ch, recv_f, fs_sem, fr_sem).wait_send()
        for i in range(1, nm):
            pltpu.make_async_remote_copy(
                part.at[ch], recv_i.at[ch, i - 1], is_sem.at[ch, i - 1], ir_sem.at[ch, i - 1],
                device_id=(band, lax.rem(mem + i, nm)), device_id_type=MESH,
            ).wait_send()
        rest(send_b, ch, recv_b, bs_sem, br_sem).wait_send()
    for r in range(8):
        pltpu.make_async_copy(spec32.at[r], prod_out.at[r], out_sem.at[r]).wait()


def body_b(inc_ref, prod_ref, inc_out, prod_out):
    @pl.when(pl.program_id(0) == 0)
    def _():
        inc_out[...] = inc_ref[...]

    for c in range(2):
        prod_out[c, 0] = prod_ref[0, c * 64 : (c + 1) * 64].reshape(32, 2, 512)


def body(coef, perturb, weight, table, wave_map, lat_map):
    wave_map, lat_map, coef, perturb, weight, table = [
        pltpu.with_memory_space_constraint(v, pltpu.HBM)
        for v in (wave_map, lat_map, coef, perturb, weight, table)
    ]
    hbm = pl.BlockSpec(memory_space=pltpu.HBM)
    smem = pl.BlockSpec(memory_space=pltpu.SMEM)
    dma = pltpu.SemaphoreType.DMA
    inc, product = pl.pallas_call(
        body_a,
        out_shape=(
            jax.ShapeDtypeStruct((12, 2, 1536), F32),
            jax.ShapeDtypeStruct((8, 128, 512), F32),
        ),
        in_specs=[smem, smem, hbm, hbm, hbm, hbm],
        out_specs=(pl.BlockSpec(memory_space=pltpu.VMEM), pl.BlockSpec(memory_space=pl.ANY)),
        scratch_shapes=[
            pltpu.VMEM((8, 512, 768), BF16),
            pltpu.VMEM((2, 8, 32, 2, 512), F32),
            pltpu.VMEM((12, 32, 2, 1536), BF16),
            pltpu.VMEM((12, 2, 1536), F32),
            pltpu.VMEM((8, 128, 512), F32),
            pltpu.VMEM((768, 8, 128), F32),
            pltpu.VMEM((NCH, 64, 16, 256), BF16),
            pltpu.VMEM((NCH, 64, 16, 256), BF16),
            pltpu.VMEM((256, 1024), BF16),
            pltpu.VMEM((1024, 1536), BF16),
            pltpu.VMEM((12, 64, 1536), F32),
            pltpu.VMEM((NCH, 8, 1536), F32),
            pltpu.VMEM((NCH, 8, 1536), F32),
            pltpu.VMEM((NCH, 3, 8, 1536), F32),
            pltpu.VMEM((24, 1536), F32),
            pltpu.VMEM((256, 1536), BF16),
            pltpu.VMEM((NCH, 64, 16, 256), BF16),
            pltpu.VMEM((NCH, 64, 16, 256), BF16),
            pltpu.VMEM((768, 768), BF16),
            pltpu.VMEM((256, 8, 128), F32),
            dma((3,)),
            dma((8,)),
            dma((NCH,)),
            dma((NCH,)),
            dma((NCH, 3)),
            dma((NCH, 3)),
            dma((NCH,)),
            dma((NCH,)),
            dma((2 * NCH,)),
            dma((8,)),
        ],
        compiler_params=pltpu.CompilerParams(
            collective_id=0, has_side_effects=True, vmem_limit_bytes=44 * 1024 * 1024
        ),
        name="transforms",
    )(wave_map, lat_map, coef, perturb, weight, table)
    whole = pl.BlockSpec((12, 2, 1536), lambda r: (0, 0, 0))
    return pl.pallas_call(
        body_b,
        out_shape=(
            jax.ShapeDtypeStruct((12, 2, 1536), F32),
            jax.ShapeDtypeStruct((2, 8, 32, 2, 512), F32),
        ),
        grid=(8,),
        in_specs=[whole, pl.BlockSpec((1, 128, 512), lambda r: (r, 0, 0))],
        out_specs=(whole, pl.BlockSpec((2, 1, 32, 2, 512), lambda r: (0, r, 0, 0, 0))),
        compiler_params=pltpu.CompilerParams(vmem_limit_bytes=16 * 1024 * 1024),
        name="place",
    )(inc, product)


def solution(mesh):
    in_specs = (
        P(None, "band", "mem", None, None),
        P("band", "mem", None, None),
        P("band", None, None),
        P("band", None, None),
        P(),
        P(),
    )
    out_specs = (P("band", None, None), P(None, "band", "mem", None, None))
    return jax.shard_map(body, mesh=mesh, in_specs=in_specs, out_specs=out_specs, check_vma=False)
```

```python
import functools
import math

import jax
import jax.numpy as jnp
from jax import lax
from jax.experimental import pallas as pl
from jax.experimental.pallas import tpu as pltpu
from jax.sharding import PartitionSpec as P

MESH = pl.DeviceIdType.MESH
F32 = jnp.float32
BF16 = jnp.bfloat16

NCH = 3


def body_a(
    wave_ref, lat_ref, coef_hbm, pert_hbm, w_hbm, table_hbm,
    inc_out, prod_out,
    tab_v, coef_v, pert_v, w_v, spec32, nat, send_f, recv_f, xt, dft, pert32, w8, part, recv_i, inc_v, adj, send_b,
    recv_b, pick, opened, held, in_sem, coef_sem, tab_sem, fs_sem, fr_sem, is_sem, ir_sem, bs_sem, br_sem, loc_sem,
):
    band = lax.axis_index("band")
    mem = lax.axis_index("mem")
    nb, nm = 64, 4
    nwave, nlat, lon = 512, 768, 1536

    tcopies = [
        pltpu.make_async_copy(table_hbm.at[r], tab_v.at[r], tab_sem.at[r]) for r in range(8)
    ]
    ccopies = [
        pltpu.make_async_copy(coef_hbm.at[:, r], coef_v.at[:, r], coef_sem.at[r]) for r in range(8)
    ]
    p_copy = pltpu.make_async_copy(pert_hbm, pert_v, in_sem.at[1])
    w_copy = pltpu.make_async_copy(w_hbm, w_v, in_sem.at[2])
    for r in range(8):
        ccopies[r].start()
        tcopies[r].start()
    p_copy.start()
    w_copy.start()

    barrier = pltpu.get_barrier_semaphore()

    def greet(i, c):
        dz = 4 + jnp.where(i // 8 % 2 == 0, -(i // 16), i // 16 + 1)
        e = lax.rem(band + dz * 8 + 7 - lax.rem(i, 8), nb)
        pl.semaphore_signal(barrier, inc=1, device_id=(e, mem), device_id_type=MESH)
        return c

    lax.fori_loop(0, nb - 1, greet, 0)
    for i in range(1, nm):
        pl.semaphore_signal(
            barrier, inc=1, device_id=(band, lax.rem(mem + i, nm)), device_id_type=MESH
        )

    z, y, x = band // 8, lax.rem(band // 4, 2), lax.rem(band, 4)

    def peer(i):
        a, b = lax.rem(i, 8), 7 - i // 8
        dz = jnp.where(lax.rem(a, 2) == 0, 4 - a // 2, 5 + a // 2)
        dz = jnp.where(a == 7, 0, dz)
        dy, dx = b // 4, lax.rem(b, 4)
        return (lax.rem(z + dz, 8) * 2 + lax.rem(y + dy, 2)) * 4 + lax.rem(x + dx, 4)

    lane_j = lax.broadcasted_iota(jnp.int32, (64, nwave), 1)

    def to_spec(r):
        keep = lane_j < nwave - wave_ref[band * 8 + r]
        for c in range(2):
            spec32[r, c * 64 : (c + 1) * 64, :] = jnp.where(
                keep, coef_v[c, r].reshape(64, nwave), 0.0
            )

    def turn(r):
        nat.reshape(nlat * 8, 128)[pl.ds(r, nlat, stride=8), :] = held[r % 2].T

    ccopies[0].wait()
    to_spec(0)
    for r in range(8):
        if r < 7:
            ccopies[r + 1].wait()
        tcopies[r].wait()
        if r < 7:
            to_spec(r + 1)
        held[r % 2] = jnp.dot(spec32[r].astype(BF16), tab_v[r], preferred_element_type=F32)
        if r > 0:
            turn(r - 1)
    turn(7)

    pl.semaphore_wait(barrier, nb - 1 + nm - 1)

    lane = lax.broadcasted_iota(jnp.int32, (8, 128), 1)
    left = lane < 64

    def send_chunk(buf, ch, dst, s_sem, r_sem):
        def one(i, c):
            e = peer(i)
            pltpu.make_async_remote_copy(
                buf.at[ch, e], dst.at[ch, band], s_sem.at[ch], r_sem.at[ch],
                device_id=(e, mem), device_id_type=MESH,
            ).start()
            return c

        lax.fori_loop(0, nb - 1, one, 0)

    def rest(buf, ch, dst, s_sem, r_sem):
        return pltpu.make_async_remote_copy(
            buf.at[ch, pl.ds(0, nb - 1)], dst.at[ch, pl.ds(0, nb - 1)], s_sem.at[ch], r_sem.at[ch],
            device_id=(lax.rem(band + 1, nb), mem), device_id_type=MESH,
        )

    def row(s):
        return nat[lat_ref[s]]

    for ch in range(NCH):

        def build(i):
            e = peer(i)
            for p in range(2):
                s0 = e * 12 + ch * 4 + 2 * p
                a, b = row(s0), row(s0 + 1)
                lo = jnp.where(left, a, pltpu.roll(b, 64, 1))
                hi = jnp.where(left, pltpu.roll(a, 64, 1), b)
                send_f[ch, e, :, p * 128 : (p + 1) * 128] = jnp.concatenate(
                    [lo, hi], axis=0
                ).astype(BF16)

        def send(i):
            e = peer(i)
            pltpu.make_async_remote_copy(
                send_f.at[ch, e], recv_f.at[ch, band], fs_sem.at[ch], fr_sem.at[ch],
                device_id=(e, mem), device_id_type=MESH,
            ).start()

        def step(g, c):
            for k in range(4):
                build(4 * g + k)
            for k in range(4):
                send(4 * g - 4 + k)
            return c

        for k in range(4):
            build(k)
        lax.fori_loop(1, nb // 4, step, 0)
        for k in range(3):
            send(nb - 4 + k)
        pltpu.make_async_copy(send_f.at[ch, band], recv_f.at[ch, band], loc_sem.at[ch]).start()

    row8 = lax.broadcasted_iota(jnp.int32, (8, 128), 0)

    def fourier(d, c):
        m = jnp.zeros((8, 128), jnp.int32)
        for i in range(8):
            m = jnp.where(row8 == i, wave_ref[d * 8 + i], m)
        low = lax.rem(m * lane, lon).astype(F32) * (2.0 * math.pi / lon)
        high = (lax.rem(m * lane, 12) * 128).astype(F32) * (2.0 * math.pi / lon)
        cb, sb = jnp.cos(low), jnp.sin(low)
        f = jnp.where(m == 0, 1.0, 2.0)
        fc, fs = f * jnp.cos(high), f * jnp.sin(high)
        for xb in range(12):
            ca = jnp.broadcast_to(fc[:, xb : xb + 1], (8, 128))
            sa = jnp.broadcast_to(fs[:, xb : xb + 1], (8, 128))
            dft[pl.ds(pl.multiple_of(d * 16, 16), 16), xb * 128 : (xb + 1) * 128] = (
                jnp.concatenate([ca * cb - sa * sb, -(sa * cb + ca * sb)], axis=0).astype(BF16)
            )
        return c

    lax.fori_loop(0, nb, fourier, 0, unroll=2)

    p_copy.wait()
    w_copy.wait()

    def to_rows(s, c):
        for k in range(32):
            pert32[s, pl.ds(2 * k, 2), :] = pert_v[s, k].astype(F32)
        return c

    lax.fori_loop(0, 12, to_rows, 0)
    for s in range(12):
        w8[s // 4, pl.ds(2 * (s % 4), 2), :] = w_v[s]

    scale = 1.0 / math.sqrt(32 * nm - 1)
    xw = 512

    for ch in range(NCH):
        pltpu.make_async_copy(send_f.at[ch, band], recv_f.at[ch, band], loc_sem.at[ch]).wait()
        rest(send_f, ch, recv_f, fs_sem, fr_sem).wait_recv()
        xt[...] = recv_f[ch].reshape(1024, 256).T

        def forward(i, c):
            cols = pl.ds(pl.multiple_of(i * xw, xw), xw)
            g = jnp.dot(xt[...], dft[:, cols], preferred_element_type=F32)
            for s in range(4):
                t = pert32[ch * 4 + s, :, cols] * g[s * 64 : (s + 1) * 64]
                t = jnp.sum(t.reshape(8, 8, xw), axis=0)
                t = t + pltpu.roll(t, 4, 0)
                t = t + pltpu.roll(t, 6, 0)
                part[ch, pl.ds(2 * s, 2), cols] = t[0:2]
            return c

        lax.fori_loop(0, lon // xw, forward, 0)

        copies = [
            pltpu.make_async_remote_copy(
                part.at[ch], recv_i.at[ch, i - 1], is_sem.at[ch, i - 1], ir_sem.at[ch, i - 1],
                device_id=(band, lax.rem(mem + i, nm)), device_id_type=MESH,
            )
            for i in range(1, nm)
        ]
        for cp in copies:
            cp.start()
        for cp in copies:
            cp.wait_recv()
        g0, g1, g2, g3 = part[ch], recv_i[ch, 0], recv_i[ch, 1], recv_i[ch, 2]
        inc = ((g0 + g2) + (g1 + g3)) * scale
        inc_v[pl.ds(8 * ch, 8), :] = inc
        w8[ch] = w8[ch] * inc * scale

        def backward(s):
            g = w8[ch, 2 * s : 2 * s + 2, :]
            g = jnp.concatenate([g] * 4, axis=0)
            a = pert32[ch * 4 + s].reshape(8, 8, lon) * g[None]
            adj[s * 64 : (s + 1) * 64, :] = a.reshape(64, lon).astype(BF16)

        for s in range(4):
            backward(s)

        def back(i, c):
            rows = pl.ds(pl.multiple_of(i * 256, 256), 256)
            v = lax.dot_general(
                dft[rows, :], adj[...], (((1,), (1,)), ((), ())), preferred_element_type=F32
            )
            send_b[ch, pl.ds(pl.multiple_of(i * 16, 16), 16)] = v.astype(BF16).reshape(16, 16, 256)
            return c

        lax.fori_loop(0, 4, back, 0)
        pltpu.make_async_copy(
            send_b.at[ch, band], recv_b.at[ch, band], loc_sem.at[NCH + ch]
        ).start()
        send_chunk(send_b, ch, recv_b, bs_sem, br_sem)

    for s in range(12):
        inc_out[s] = inc_v[pl.ds(2 * s, 2), :]

    def select(t, c):
        halves = []
        for h in range(2):
            m = jnp.zeros((8, 128), jnp.int32)
            for i in range(8):
                k = h * 8 + i
                m = jnp.where(row8 == i, lat_ref[(t % 16 * 4 + k // 4) * 12 + t // 16 * 4 + k % 4], m)
            halves.append(m)
        m = jnp.concatenate(halves, axis=0)
        lane16 = lax.broadcasted_iota(jnp.int32, (16, 128), 1)
        for b in range(nlat // 128):
            pick[pl.ds(pl.multiple_of(t * 16, 16), 16), b * 128 : (b + 1) * 128] = jnp.where(
                m == lane16 + b * 128, 1.0, 0.0
            ).astype(BF16)
        return c

    lax.fori_loop(0, nlat // 16, select, 0, unroll=2)

    def arrange(r, c):
        tab_v[r] = lax.dot_general(
            tab_v[r], pick[...], (((1,), (1,)), ((), ())), preferred_element_type=F32
        ).astype(BF16)
        return c

    lax.fori_loop(0, 8, arrange, 0)

    for ch in range(NCH):
        pltpu.make_async_copy(
            send_b.at[ch, band], recv_b.at[ch, band], loc_sem.at[NCH + ch]
        ).wait()
        rest(send_b, ch, recv_b, bs_sem, br_sem).wait_recv()

        def open_up(g, c):
            for k in range(8):
                e = g * 8 + k
                for p in range(2):
                    t = recv_b[ch, e, :, p * 128 : (p + 1) * 128].astype(F32)
                    lo, hi = t[0:8], t[8:16]
                    opened[e * 4 + 2 * p] = jnp.where(left, lo, pltpu.roll(hi, 64, 1))
                    opened[e * 4 + 2 * p + 1] = jnp.where(left, pltpu.roll(lo, 64, 1), hi)
            return c

        lax.fori_loop(0, nb // 8, open_up, 0)

        for r in range(8):
            a = opened.reshape(2048, 128)[pl.ds(r, 256, stride=8), :].astype(BF16)
            v = lax.dot_general(
                a, tab_v[r, :, ch * 256 : (ch + 1) * 256], (((0,), (1,)), ((), ())),
                preferred_element_type=F32,
            )
            if ch < NCH - 1:
                spec32[r] += v
            else:
                keep = lax.broadcasted_iota(jnp.int32, (128, nwave), 1) < nwave - wave_ref[band * 8 + r]
                prod_out[r] = jnp.where(keep, spec32[r] + v, 0.0)

    for ch in range(NCH):
        rest(send_f, ch, recv_f, fs_sem, fr_sem).wait_send()
        for i in range(1, nm):
            pltpu.make_async_remote_copy(
                part.at[ch], recv_i.at[ch, i - 1], is_sem.at[ch, i - 1], ir_sem.at[ch, i - 1],
                device_id=(band, lax.rem(mem + i, nm)), device_id_type=MESH,
            ).wait_send()
        rest(send_b, ch, recv_b, bs_sem, br_sem).wait_send()


def body_b(inc_ref, prod_ref, inc_out, prod_out):
    @pl.when(pl.program_id(0) == 0)
    def _():
        inc_out[...] = inc_ref[...]

    for c in range(2):
        for r in range(4):
            prod_out[c, r] = prod_ref[r, c * 64 : (c + 1) * 64].reshape(32, 2, 512)


def body(coef, perturb, weight, table, wave_map, lat_map):
    wave_map, lat_map, coef, perturb, weight, table = [
        pltpu.with_memory_space_constraint(v, pltpu.HBM)
        for v in (wave_map, lat_map, coef, perturb, weight, table)
    ]
    hbm = pl.BlockSpec(memory_space=pltpu.HBM)
    smem = pl.BlockSpec(memory_space=pltpu.SMEM)
    dma = pltpu.SemaphoreType.DMA
    inc, product = pl.pallas_call(
        body_a,
        out_shape=(
            jax.ShapeDtypeStruct((12, 2, 1536), F32),
            jax.ShapeDtypeStruct((8, 128, 512), F32),
        ),
        in_specs=[smem, smem, hbm, hbm, hbm, hbm],
        out_specs=(pl.BlockSpec(memory_space=pltpu.VMEM), pl.BlockSpec(memory_space=pltpu.VMEM)),
        scratch_shapes=[
            pltpu.VMEM((8, 512, 768), BF16),
            pltpu.VMEM((2, 8, 32, 2, 512), F32),
            pltpu.VMEM((12, 32, 2, 1536), BF16),
            pltpu.VMEM((12, 2, 1536), F32),
            pltpu.VMEM((8, 128, 512), F32),
            pltpu.VMEM((768, 8, 128), F32),
            pltpu.VMEM((NCH, 64, 16, 256), BF16),
            pltpu.VMEM((NCH, 64, 16, 256), BF16),
            pltpu.VMEM((256, 1024), BF16),
            pltpu.VMEM((1024, 1536), BF16),
            pltpu.VMEM((12, 64, 1536), F32),
            pltpu.VMEM((NCH, 8, 1536), F32),
            pltpu.VMEM((NCH, 8, 1536), F32),
            pltpu.VMEM((NCH, 3, 8, 1536), F32),
            pltpu.VMEM((24, 1536), F32),
            pltpu.VMEM((256, 1536), BF16),
            pltpu.VMEM((NCH, 64, 16, 256), BF16),
            pltpu.VMEM((NCH, 64, 16, 256), BF16),
            pltpu.VMEM((768, 768), BF16),
            pltpu.VMEM((256, 8, 128), F32),
            pltpu.VMEM((2, 128, 768), F32),
            dma((3,)),
            dma((8,)),
            dma((8,)),
            dma((NCH,)),
            dma((NCH,)),
            dma((NCH, 3)),
            dma((NCH, 3)),
            dma((NCH,)),
            dma((NCH,)),
            dma((2 * NCH,)),
        ],
        compiler_params=pltpu.CompilerParams(
            collective_id=0, has_side_effects=True, vmem_limit_bytes=44 * 1024 * 1024
        ),
        name="transforms",
    )(wave_map, lat_map, coef, perturb, weight, table)
    whole = pl.BlockSpec((12, 2, 1536), lambda r: (0, 0, 0))
    return pl.pallas_call(
        body_b,
        out_shape=(
            jax.ShapeDtypeStruct((12, 2, 1536), F32),
            jax.ShapeDtypeStruct((2, 8, 32, 2, 512), F32),
        ),
        grid=(2,),
        in_specs=[whole, pl.BlockSpec((4, 128, 512), lambda r: (r, 0, 0))],
        out_specs=(whole, pl.BlockSpec((2, 4, 32, 2, 512), lambda r: (0, r, 0, 0, 0))),
        compiler_params=pltpu.CompilerParams(vmem_limit_bytes=16 * 1024 * 1024),
        name="place",
    )(inc, product)


def solution(mesh):
    in_specs = (
        P(None, "band", "mem", None, None),
        P("band", "mem", None, None),
        P("band", None, None),
        P("band", None, None),
        P(),
        P(),
    )
    out_specs = (P("band", None, None), P(None, "band", "mem", None, None))
    return jax.shard_map(body, mesh=mesh, in_specs=in_specs, out_specs=out_specs, check_vma=False)
```

```python
import functools
import math

import jax
import jax.numpy as jnp
from jax import lax
from jax.experimental import pallas as pl
from jax.experimental.pallas import tpu as pltpu
from jax.sharding import PartitionSpec as P

MESH = pl.DeviceIdType.MESH
F32 = jnp.float32
BF16 = jnp.bfloat16

NCH = 3
STAGES = ((0, 0, 1), (1, 0, 1), (2, 0, 2), (2, 1, 2))
NST = len(STAGES)


def body_a(
    wave_ref, lat_ref, coef_hbm, pert_hbm, w_hbm, table_hbm,
    inc_out, prod_out,
    tab_v, coef_v, pert_v, w_v, spec32, nat, send_f, recv_f, xt, dft, pert32, w8, part, recv_i, inc_v, adj, send_b,
    recv_b, pick, opened, held, in_sem, coef_sem, tab_sem, fs_sem, fr_sem, is_sem, ir_sem, bs_sem, br_sem, loc_sem,
):
    band = lax.axis_index("band")
    mem = lax.axis_index("mem")
    nb, nm = 64, 4
    nwave, nlat, lon = 512, 768, 1536

    tcopies = [
        pltpu.make_async_copy(table_hbm.at[r], tab_v.at[r], tab_sem.at[r]) for r in range(8)
    ]
    ccopies = [
        pltpu.make_async_copy(coef_hbm.at[:, r], coef_v.at[:, r], coef_sem.at[r]) for r in range(8)
    ]
    p_copy = pltpu.make_async_copy(pert_hbm, pert_v, in_sem.at[1])
    w_copy = pltpu.make_async_copy(w_hbm, w_v, in_sem.at[2])
    for r in range(8):
        ccopies[r].start()
        tcopies[r].start()
    p_copy.start()
    w_copy.start()

    barrier = pltpu.get_barrier_semaphore()

    def greet(i, c):
        dz = 4 + jnp.where(i // 8 % 2 == 0, -(i // 16), i // 16 + 1)
        e = lax.rem(band + dz * 8 + 7 - lax.rem(i, 8), nb)
        pl.semaphore_signal(barrier, inc=1, device_id=(e, mem), device_id_type=MESH)
        return c

    lax.fori_loop(0, nb - 1, greet, 0)
    for i in range(1, nm):
        pl.semaphore_signal(
            barrier, inc=1, device_id=(band, lax.rem(mem + i, nm)), device_id_type=MESH
        )

    z, y, x = band // 8, lax.rem(band // 4, 2), lax.rem(band, 4)

    def peer(i):
        a, b = lax.rem(i, 8), 7 - i // 8
        dz = jnp.where(lax.rem(a, 2) == 0, 4 - a // 2, 5 + a // 2)
        dz = jnp.where(a == 7, 0, dz)
        dy, dx = b // 4, lax.rem(b, 4)
        return (lax.rem(z + dz, 8) * 2 + lax.rem(y + dy, 2)) * 4 + lax.rem(x + dx, 4)

    lane_j = lax.broadcasted_iota(jnp.int32, (64, nwave), 1)

    def to_spec(r):
        keep = lane_j < nwave - wave_ref[band * 8 + r]
        for c in range(2):
            spec32[r, c * 64 : (c + 1) * 64, :] = jnp.where(
                keep, coef_v[c, r].reshape(64, nwave), 0.0
            )

    def turn(r):
        nat.reshape(nlat * 8, 128)[pl.ds(r, nlat, stride=8), :] = held[r % 2].T

    ccopies[0].wait()
    to_spec(0)
    for r in range(8):
        if r < 7:
            ccopies[r + 1].wait()
        tcopies[r].wait()
        if r < 7:
            to_spec(r + 1)
        held[r % 2] = jnp.dot(spec32[r].astype(BF16), tab_v[r], preferred_element_type=F32)
        if r > 0:
            turn(r - 1)
    turn(7)

    pl.semaphore_wait(barrier, nb - 1 + nm - 1)

    lane = lax.broadcasted_iota(jnp.int32, (8, 128), 1)
    left = lane < 64

    def rest(buf, ch, dst, s_sem, r_sem):
        return pltpu.make_async_remote_copy(
            buf.at[ch, pl.ds(0, nb - 1)], dst.at[ch, pl.ds(0, nb - 1)], s_sem.at[ch], r_sem.at[ch],
            device_id=(lax.rem(band + 1, nb), mem), device_id_type=MESH,
        )

    def own_back(ch):
        return pltpu.make_async_copy(
            send_b.at[ch, band], recv_b.at[ch, band], loc_sem.at[NCH + ch]
        )

    def stage_of(st):
        ch, half, halves = STAGES[st]
        lo = half * 32
        return ch, lo, nb - 1 if half == halves - 1 else 32

    def send_back(st):
        ch, lo, hi = stage_of(st)

        def one(i, c):
            e = peer(i)
            pltpu.make_async_remote_copy(
                send_b.at[ch, e], recv_b.at[ch, band], bs_sem.at[st], br_sem.at[st],
                device_id=(e, mem), device_id_type=MESH,
            ).start()
            return c

        lax.fori_loop(lo, hi, one, 0)

    def rest_back(st):
        ch, lo, hi = stage_of(st)
        return pltpu.make_async_remote_copy(
            send_b.at[ch, pl.ds(0, hi - lo)], recv_b.at[ch, pl.ds(0, hi - lo)],
            bs_sem.at[st], br_sem.at[st],
            device_id=(lax.rem(band + 1, nb), mem), device_id_type=MESH,
        )

    def source(st, n):
        if STAGES[st][2] == 1:
            return n
        side = 1 - y if STAGES[st][1] == 0 else y
        return n // 4 * 8 + side * 4 + n % 4

    def row(s):
        return nat[lat_ref[s]]

    for ch in range(NCH):

        def build(i):
            e = peer(i)
            for p in range(2):
                s0 = e * 12 + ch * 4 + 2 * p
                a, b = row(s0), row(s0 + 1)
                lo = jnp.where(left, a, pltpu.roll(b, 64, 1))
                hi = jnp.where(left, pltpu.roll(a, 64, 1), b)
                send_f[ch, e, :, p * 128 : (p + 1) * 128] = jnp.concatenate(
                    [lo, hi], axis=0
                ).astype(BF16)

        def send(i):
            e = peer(i)
            pltpu.make_async_remote_copy(
                send_f.at[ch, e], recv_f.at[ch, band], fs_sem.at[ch], fr_sem.at[ch],
                device_id=(e, mem), device_id_type=MESH,
            ).start()

        def step(g, c):
            for k in range(4):
                build(4 * g + k)
            for k in range(4):
                send(4 * g - 4 + k)
            return c

        for k in range(4):
            build(k)
        lax.fori_loop(1, nb // 4, step, 0)
        for k in range(3):
            send(nb - 4 + k)
        pltpu.make_async_copy(send_f.at[ch, band], recv_f.at[ch, band], loc_sem.at[ch]).start()

    row8 = lax.broadcasted_iota(jnp.int32, (8, 128), 0)

    def fourier(d, c):
        m = jnp.zeros((8, 128), jnp.int32)
        for i in range(8):
            m = jnp.where(row8 == i, wave_ref[d * 8 + i], m)
        low = lax.rem(m * lane, lon).astype(F32) * (2.0 * math.pi / lon)
        high = (lax.rem(m * lane, 12) * 128).astype(F32) * (2.0 * math.pi / lon)
        cb, sb = jnp.cos(low), jnp.sin(low)
        f = jnp.where(m == 0, 1.0, 2.0)
        fc, fs = f * jnp.cos(high), f * jnp.sin(high)
        for xb in range(12):
            ca = jnp.broadcast_to(fc[:, xb : xb + 1], (8, 128))
            sa = jnp.broadcast_to(fs[:, xb : xb + 1], (8, 128))
            dft[pl.ds(pl.multiple_of(d * 16, 16), 16), xb * 128 : (xb + 1) * 128] = (
                jnp.concatenate([ca * cb - sa * sb, -(sa * cb + ca * sb)], axis=0).astype(BF16)
            )
        return c

    lax.fori_loop(0, nb, fourier, 0, unroll=2)

    p_copy.wait()
    w_copy.wait()

    def to_rows(s, c):
        for k in range(32):
            pert32[s, pl.ds(2 * k, 2), :] = pert_v[s, k].astype(F32)
        return c

    lax.fori_loop(0, 12, to_rows, 0)
    for s in range(12):
        w8[s // 4, pl.ds(2 * (s % 4), 2), :] = w_v[s]

    scale = 1.0 / math.sqrt(32 * nm - 1)
    xw = 512

    for ch in range(NCH):
        pltpu.make_async_copy(send_f.at[ch, band], recv_f.at[ch, band], loc_sem.at[ch]).wait()
        rest(send_f, ch, recv_f, fs_sem, fr_sem).wait_recv()
        xt[...] = recv_f[ch].reshape(1024, 256).T

        def forward(i, c):
            cols = pl.ds(pl.multiple_of(i * xw, xw), xw)
            g = jnp.dot(xt[...], dft[:, cols], preferred_element_type=F32)
            for s in range(4):
                t = pert32[ch * 4 + s, :, cols] * g[s * 64 : (s + 1) * 64]
                t = jnp.sum(t.reshape(8, 8, xw), axis=0)
                t = t + pltpu.roll(t, 4, 0)
                t = t + pltpu.roll(t, 6, 0)
                part[ch, pl.ds(2 * s, 2), cols] = t[0:2]
            return c

        lax.fori_loop(0, lon // xw, forward, 0)

        copies = [
            pltpu.make_async_remote_copy(
                part.at[ch], recv_i.at[ch, i - 1], is_sem.at[ch, i - 1], ir_sem.at[ch, i - 1],
                device_id=(band, lax.rem(mem + i, nm)), device_id_type=MESH,
            )
            for i in range(1, nm)
        ]
        for cp in copies:
            cp.start()
        for cp in copies:
            cp.wait_recv()
        g0, g1, g2, g3 = part[ch], recv_i[ch, 0], recv_i[ch, 1], recv_i[ch, 2]
        inc = ((g0 + g2) + (g1 + g3)) * scale
        inc_v[pl.ds(8 * ch, 8), :] = inc
        w8[ch] = w8[ch] * inc * scale

        def backward(s):
            g = w8[ch, 2 * s : 2 * s + 2, :]
            g = jnp.concatenate([g] * 4, axis=0)
            a = pert32[ch * 4 + s].reshape(8, 8, lon) * g[None]
            adj[s * 64 : (s + 1) * 64, :] = a.reshape(64, lon).astype(BF16)

        for s in range(4):
            backward(s)

        def back(i, c):
            rows = pl.ds(pl.multiple_of(i * 256, 256), 256)
            v = lax.dot_general(
                dft[rows, :], adj[...], (((1,), (1,)), ((), ())), preferred_element_type=F32
            )
            send_b[ch, pl.ds(pl.multiple_of(i * 16, 16), 16)] = v.astype(BF16).reshape(16, 16, 256)
            return c

        lax.fori_loop(0, 4, back, 0)
        for st in range(NST):
            if STAGES[st][0] == ch:
                send_back(st)
        own_back(ch).start()

    for s in range(12):
        inc_out[s] = inc_v[pl.ds(2 * s, 2), :]

    lane16 = lax.broadcasted_iota(jnp.int32, (16, 128), 1)
    first = 0
    firsts = []
    for st, (ch, _, halves_of) in enumerate(STAGES):
        firsts.append(first)

        def choose(t, c, st=st, ch=ch, first=first):
            halves = []
            for h in range(2):
                m = jnp.zeros((8, 128), jnp.int32)
                for i in range(8):
                    k = h * 8 + i
                    s = source(st, t * 4 + k // 4) * 12 + ch * 4 + k % 4
                    m = jnp.where(row8 == i, lat_ref[s], m)
                halves.append(m)
            m = jnp.concatenate(halves, axis=0)
            for b in range(nlat // 128):
                pick[pl.ds(pl.multiple_of(first + t * 16, 16), 16), b * 128 : (b + 1) * 128] = (
                    jnp.where(m == lane16 + b * 128, 1.0, 0.0).astype(BF16)
                )
            return c

        lax.fori_loop(0, nb // 4 // halves_of, choose, 0, unroll=2)
        first += nb * 4 // halves_of

    def arrange(r, c):
        tab_v[r] = lax.dot_general(
            tab_v[r], pick[...], (((1,), (1,)), ((), ())), preferred_element_type=F32
        ).astype(BF16)
        return c

    lax.fori_loop(0, 8, arrange, 0)

    for st, (ch, half, halves_of) in enumerate(STAGES):
        if half == halves_of - 1:
            own_back(ch).wait()
        rest_back(st).wait_recv()
        depth = nb * 4 // halves_of

        def open_up(g, c, st=st, ch=ch):
            for k in range(8):
                n = g * 8 + k
                e = source(st, n)
                for p in range(2):
                    t = recv_b[ch, e, :, p * 128 : (p + 1) * 128].astype(F32)
                    lo, hi = t[0:8], t[8:16]
                    opened[n * 4 + 2 * p] = jnp.where(left, lo, pltpu.roll(hi, 64, 1))
                    opened[n * 4 + 2 * p + 1] = jnp.where(left, pltpu.roll(lo, 64, 1), hi)
            return c

        lax.fori_loop(0, nb // 8 // halves_of, open_up, 0)

        for r in range(8):
            a = opened.reshape(2048, 128)[pl.ds(r, depth, stride=8), :].astype(BF16)
            v = lax.dot_general(
                a, tab_v[r, :, firsts[st] : firsts[st] + depth], (((0,), (1,)), ((), ())),
                preferred_element_type=F32,
            )
            if st < NST - 1:
                spec32[r] += v
            else:
                keep = lax.broadcasted_iota(jnp.int32, (128, nwave), 1) < nwave - wave_ref[band * 8 + r]
                prod_out[r] = jnp.where(keep, spec32[r] + v, 0.0)

    for ch in range(NCH):
        rest(send_f, ch, recv_f, fs_sem, fr_sem).wait_send()
        for i in range(1, nm):
            pltpu.make_async_remote_copy(
                part.at[ch], recv_i.at[ch, i - 1], is_sem.at[ch, i - 1], ir_sem.at[ch, i - 1],
                device_id=(band, lax.rem(mem + i, nm)), device_id_type=MESH,
            ).wait_send()
    for st in range(NST):
        rest_back(st).wait_send()


def body_b(inc_ref, prod_ref, inc_out, prod_out):
    @pl.when(pl.program_id(0) == 0)
    def _():
        inc_out[...] = inc_ref[...]

    for c in range(2):
        for r in range(4):
            prod_out[c, r] = prod_ref[r, c * 64 : (c + 1) * 64].reshape(32, 2, 512)


def body(coef, perturb, weight, table, wave_map, lat_map):
    wave_map, lat_map, coef, perturb, weight, table = [
        pltpu.with_memory_space_constraint(v, pltpu.HBM)
        for v in (wave_map, lat_map, coef, perturb, weight, table)
    ]
    hbm = pl.BlockSpec(memory_space=pltpu.HBM)
    smem = pl.BlockSpec(memory_space=pltpu.SMEM)
    dma = pltpu.SemaphoreType.DMA
    inc, product = pl.pallas_call(
        body_a,
        out_shape=(
            jax.ShapeDtypeStruct((12, 2, 1536), F32),
            jax.ShapeDtypeStruct((8, 128, 512), F32),
        ),
        in_specs=[smem, smem, hbm, hbm, hbm, hbm],
        out_specs=(pl.BlockSpec(memory_space=pltpu.VMEM), pl.BlockSpec(memory_space=pltpu.VMEM)),
        scratch_shapes=[
            pltpu.VMEM((8, 512, 768), BF16),
            pltpu.VMEM((2, 8, 32, 2, 512), F32),
            pltpu.VMEM((12, 32, 2, 1536), BF16),
            pltpu.VMEM((12, 2, 1536), F32),
            pltpu.VMEM((8, 128, 512), F32),
            pltpu.VMEM((768, 8, 128), F32),
            pltpu.VMEM((NCH, 64, 16, 256), BF16),
            pltpu.VMEM((NCH, 64, 16, 256), BF16),
            pltpu.VMEM((256, 1024), BF16),
            pltpu.VMEM((1024, 1536), BF16),
            pltpu.VMEM((12, 64, 1536), F32),
            pltpu.VMEM((NCH, 8, 1536), F32),
            pltpu.VMEM((NCH, 8, 1536), F32),
            pltpu.VMEM((NCH, 3, 8, 1536), F32),
            pltpu.VMEM((24, 1536), F32),
            pltpu.VMEM((256, 1536), BF16),
            pltpu.VMEM((NCH, 64, 16, 256), BF16),
            pltpu.VMEM((NCH, 64, 16, 256), BF16),
            pltpu.VMEM((768, 768), BF16),
            pltpu.VMEM((256, 8, 128), F32),
            pltpu.VMEM((2, 128, 768), F32),
            dma((3,)),
            dma((8,)),
            dma((8,)),
            dma((NCH,)),
            dma((NCH,)),
            dma((NCH, 3)),
            dma((NCH, 3)),
            dma((NST,)),
            dma((NST,)),
            dma((2 * NCH,)),
        ],
        compiler_params=pltpu.CompilerParams(
            collective_id=0, has_side_effects=True, vmem_limit_bytes=44 * 1024 * 1024
        ),
        name="transforms",
    )(wave_map, lat_map, coef, perturb, weight, table)
    whole = pl.BlockSpec((12, 2, 1536), lambda r: (0, 0, 0))
    return pl.pallas_call(
        body_b,
        out_shape=(
            jax.ShapeDtypeStruct((12, 2, 1536), F32),
            jax.ShapeDtypeStruct((2, 8, 32, 2, 512), F32),
        ),
        grid=(2,),
        in_specs=[whole, pl.BlockSpec((4, 128, 512), lambda r: (r, 0, 0))],
        out_specs=(whole, pl.BlockSpec((2, 4, 32, 2, 512), lambda r: (0, r, 0, 0, 0))),
        compiler_params=pltpu.CompilerParams(vmem_limit_bytes=16 * 1024 * 1024),
        name="place",
    )(inc, product)


def solution(mesh):
    in_specs = (
        P(None, "band", "mem", None, None),
        P("band", "mem", None, None),
        P("band", None, None),
        P("band", None, None),
        P(),
        P(),
    )
    out_specs = (P("band", None, None), P(None, "band", "mem", None, None))
    return jax.shard_map(body, mesh=mesh, in_specs=in_specs, out_specs=out_specs, check_vma=False)
```
